768 devices in a mesh: dp: 192 (over z, x_hi, y), section: 4 (over x_lo, core).
Axes of the slice: x: 4 (x_hi: 2, x_lo: 2; x = x_hi * 2 + x_lo), y: 8, z: 12, core: 2. Of those that a mesh axis runs over, the one named last changes fastest.
Arguments:
- hidden_input_rows: bfloat16 [4, 24576, 3584], P('section', 'dp'), may hold values from -6 to 6
- embeddings: bfloat16 [4, 24576, 3584], P('section', 'dp'), may hold values from -6 to 6
- adapter_down_weight: bfloat16 [4, 2, 64, 7168], P('section'), may hold values from -0.0625 to 0.0625
- adapter_up_weight: bfloat16 [4, 2, 64, 3584], P('section'), may hold values from -0.75 to 0.75
- shared_norm_gain: float32 [2, 7168], replicated, may hold values from 0.1 to 1.9
- plan: int32 [4, 2], P('section'), may hold values from 0 to 2
- adapter_output_cotangent: bfloat16 [4, 24576, 3584], P('section', 'dp'), may hold values from -6 to 6
Outputs:
- carried_final_rows: bfloat16 [4, 24576, 3584], P('section', 'dp')
- lora_b_grad: float32 [4, 2, 64, 3584], P('section')
- gain_grad: float32 [2, 7168], replicated
The draws below stay inside these ranges and needn't reach their ends.
Inputs may be any that keep to these rules, and one draw needn't show every extreme that they name: `plan`: an entry 2 means that the layer calls no shared block.
All inputs are finite; a program needn't handle non-finite values.
Results may differ from the reference program's by a relative error of at most 0.007.
Values may be sent and summed in bfloat16 or wider, within the bound.
No kernel may reach another device: no remote copies, remote signals or barrier semaphores. Data moves between devices by JAX's collectives and lax.ppermute only.
A program may use at most 64 MiB of HBM per device.

```python
import math
import jax
import jax.numpy as jnp
from jax import lax

MODEL_WIDTH = 3584
ADAPTER_RANK = 64
SECTION_LAYERS = 2
BLOCKS = 2
ROWS = 128
TOKENS = 24576
N_DP = 192
N_SECTION = 4


def plant(values, stream_key, smallest, largest):
    longest = values.shape.index(max(values.shape))
    spots = []
    for shift in (0, 1):
        where = [jax.random.randint(jax.random.fold_in(stream_key, axis), (), 0, length) for axis, length in enumerate(values.shape)]
        where[longest] = (where[longest] + shift) % values.shape[longest]
        spots.append(tuple(where))
    return values.at[spots[0]].set(smallest).at[spots[1]].set(largest)


def block_scale(rng, shape, split, low, top_value):
    def one(dim, blocks):
        heights = jax.random.uniform(jax.random.fold_in(jax.random.fold_in(rng, 6), dim), (blocks,), jnp.float32, low / len(split), top_value / len(split))
        return jnp.repeat(jnp.exp(heights), shape[dim] // blocks).reshape((-1,) + (1,) * (len(shape) - dim - 1))

    loudness = one(*split[0])
    for cut in split[1:]:
        loudness = loudness * one(*cut)
    return loudness


def gaussian(key, dims, width, limit, shards=(), kind=jnp.bfloat16):
    factor_of = block_scale(key, dims, shards, -0.22, 0.18) if shards else 1.0
    entries = jax.random.normal(key, dims, jnp.float32) * width * factor_of
    return jnp.minimum(jnp.maximum(entries, -limit), limit).astype(kind)


def setup_inputs(seed: int = 0) -> dict:
    key_of = jax.random.split(jax.random.key(seed), 8)
    hidden_input_rows = gaussian(key_of[0], (N_SECTION, TOKENS, MODEL_WIDTH), 1.0, 6.0, ((0, 4), (1, 192)))
    embeddings = gaussian(key_of[1], (N_SECTION, TOKENS, MODEL_WIDTH), 1.0, 6.0, ((0, 4), (1, 192)))
    adapter_down_weight = gaussian(key_of[2], (N_SECTION, SECTION_LAYERS, ADAPTER_RANK, 2 * MODEL_WIDTH), (2 * MODEL_WIDTH) ** -0.5, 0.0625, ((0, 4),))
    adapter_up_weight = gaussian(key_of[3], (N_SECTION, SECTION_LAYERS, ADAPTER_RANK, MODEL_WIDTH), ADAPTER_RANK ** -0.5, 0.75, ((0, 4),))
    shared_norm_gain = jnp.clip(1.0 + 0.18 * jax.random.normal(key_of[4], (BLOCKS, 2 * MODEL_WIDTH), jnp.float32), 0.1, 1.9)
    plan = plant(jax.random.randint(key_of[5], (N_SECTION, SECTION_LAYERS), 0, BLOCKS + 1), jax.random.fold_in(key_of[5], 1), 0, BLOCKS).astype(jnp.int32)
    adapter_output_cotangent = gaussian(key_of[6], (N_SECTION, TOKENS, MODEL_WIDTH), 1.0, 6.0, ((0, 4), (1, 192)))
    return {"hidden_input_rows": hidden_input_rows, "embeddings": embeddings, "adapter_down_weight": adapter_down_weight, "adapter_up_weight": adapter_up_weight, "shared_norm_gain": shared_norm_gain, "plan": plan, "adapter_output_cotangent": adapter_output_cotangent}


def apply_shared_block(hidden, embed_rows, down_weight_picked, up_weight_picked, gain_vector, output_cotangent):
    joined = jnp.concatenate([hidden.astype(jnp.float32), embed_rows.astype(jnp.float32)], axis=-1)
    inverse = lax.rsqrt(lax.optimization_barrier(jnp.mean(joined * joined, axis=-1, keepdims=True)) + 1e-05)
    normed = joined * inverse
    scaled = (normed * gain_vector).astype(jnp.bfloat16)
    adapter_latent = jnp.dot(scaled, down_weight_picked.T, preferred_element_type=jnp.float32).astype(jnp.bfloat16)
    update = jnp.dot(adapter_latent, up_weight_picked, preferred_element_type=jnp.float32)
    refreshed_state = (hidden.astype(jnp.float32) + update).astype(jnp.bfloat16)
    latent_grad = jnp.dot(output_cotangent, up_weight_picked.T, preferred_element_type=jnp.float32).astype(jnp.bfloat16)
    normed_grad = jnp.dot(latent_grad, down_weight_picked, preferred_element_type=jnp.float32)
    gain_gradient_piece = lax.optimization_barrier(jnp.sum(normed_grad * normed, axis=0))
    adapter_gradient_piece = jnp.dot(adapter_latent.T, output_cotangent, preferred_element_type=jnp.float32)
    return (refreshed_state, adapter_gradient_piece, gain_gradient_piece)

def per_block_apply(hidden, embed_rows, down_weight_picked, up_weight_picked, gain_vector, output_cotangent):
    shaped = (N_DP, ROWS, hidden.shape[-1])

    def one_block(loop_carry, scan_elements):
        state_refresh, adapter_gradient_piece, gain_gradient_piece = apply_shared_block(scan_elements[0], scan_elements[1], down_weight_picked, up_weight_picked, gain_vector, scan_elements[2])
        return ((loop_carry[0] + adapter_gradient_piece, loop_carry[1] + gain_gradient_piece), state_refresh)
    start = (jnp.zeros((up_weight_picked.shape[0], up_weight_picked.shape[1]), jnp.float32), jnp.zeros((down_weight_picked.shape[1],), jnp.float32))
    sums, refreshed_state = lax.scan(one_block, start, (hidden.reshape(shaped), embed_rows.reshape(shaped), output_cotangent.reshape(shaped)))
    return (refreshed_state.reshape(hidden.shape), sums[0], sums[1])

def reference(hidden_input_rows, embeddings, adapter_down_weight, adapter_up_weight, shared_norm_gain, plan, adapter_output_cotangent):
    sections = hidden_input_rows.shape[0]
    loop_states = [hidden_input_rows[index] for index in range(sections)]
    adapter_gradient_total = jnp.zeros(adapter_up_weight.shape, jnp.float32)
    gain_gradient_total = jnp.zeros(shared_norm_gain.shape, jnp.float32)
    block_ids = jnp.arange(shared_norm_gain.shape[0], dtype=jnp.int32)
    for step_id in range(sections):
        for microbatch_index in range(sections):
            layer_id = microbatch_index + step_id
            layer_position = layer_id % sections
            layer_slot_index = layer_id // sections
            block_id = plan[layer_position, layer_slot_index].astype(jnp.int32)
            block_pick = (block_ids == block_id).astype(jnp.float32)
            active = jnp.sum(block_pick)
            gain_vector = lax.optimization_barrier(jnp.sum(block_pick[:, None] * shared_norm_gain, axis=0))
            next_loop_state, adapter_gradient_piece, gain_gradient_piece = per_block_apply(loop_states[microbatch_index], embeddings[microbatch_index], adapter_down_weight[layer_position, layer_slot_index], adapter_up_weight[layer_position, layer_slot_index], gain_vector, adapter_output_cotangent[microbatch_index])
            loop_states[microbatch_index] = jnp.where(active > 0.5, next_loop_state, loop_states[microbatch_index])
            adapter_gradient_total = adapter_gradient_total.at[layer_position, layer_slot_index].add(active * adapter_gradient_piece)
            gain_gradient_total = gain_gradient_total + block_pick[:, None] * gain_gradient_piece[None, :]
    inverse_norm_scale = 1.0 / math.sqrt(TOKENS)
    carried_final_rows = jnp.stack([loop_states[(index + 1) % sections] for index in range(sections)])
    return (carried_final_rows, adapter_gradient_total * inverse_norm_scale, gain_gradient_total * inverse_norm_scale)
```

```python
import functools
import math

import jax
import jax.numpy as jnp
import numpy as np
from jax import lax
from jax.experimental import pallas as pl
from jax.experimental.pallas import tpu as pltpu
from jax.sharding import Mesh
from jax.sharding import PartitionSpec as P


F32 = jnp.float32
BF16 = jnp.bfloat16
STEP_LANES = 512
ID_LANES = 128
CONTRACT_LAST = (((1,), (1,)), ((), ()))
CONTRACT_FIRST = (((0,), (0,)), ((), ()))


def layer_kernel(own, hidden, embed, cot, gain, gain_total, *refs):
    width = hidden.shape[-1]
    if own:
        down_ref, up_ref, id_ref, state_out, grad_out, gain_out, scaled = refs

        def down(start, size):
            return down_ref[0, 0, :, start : start + size]

        def up(start, size):
            return up_ref[0, 0, :, start : start + size]

        ids = id_ref[...]
    else:
        first, second, state_out, grad_out, gain_out, scaled = refs

        def down(start, size):
            return jnp.concatenate(
                [first[:, start : start + size], second[:, start : start + size]], axis=0
            )

        def up(start, size):
            return down(2 * width + start, size)

        ids = first[0:1, 3 * width : 3 * width + ID_LANES].astype(F32)
    block_id = jnp.max(ids, axis=1, keepdims=True)
    pick_0 = (jnp.abs(block_id - 0.0) < 0.5).astype(F32)
    pick_1 = (jnp.abs(block_id - 1.0) < 0.5).astype(F32)
    active = pick_0 + pick_1

    starts = range(0, width, STEP_LANES)
    squares = jnp.zeros((hidden.shape[0], ID_LANES), F32)
    for rows in (hidden, embed):
        for start in starts:
            wide = rows[:, start : start + STEP_LANES].astype(F32)
            wide = wide * wide
            for lane in range(0, STEP_LANES, ID_LANES):
                squares = squares + wide[:, lane : lane + ID_LANES]
    squares_sum = jnp.sum(squares, axis=1, keepdims=True)
    inverse = lax.rsqrt(squares_sum / (2 * width) + 1e-05)

    latent_grad = lax.dot_general(
        cot[...], up(0, width), CONTRACT_LAST, preferred_element_type=F32
    ).astype(BF16)
    for part, rows in enumerate((hidden, embed)):
        for start in starts:
            here = part * width + start
            lanes = slice(here, here + STEP_LANES)
            normed = rows[:, start : start + STEP_LANES].astype(F32) * inverse
            gain_now = pick_0 * gain[0:1, lanes] + pick_1 * gain[1:2, lanes]
            scaled[:, lanes] = (normed * gain_now).astype(BF16)
            normed_grad = jnp.dot(
                latent_grad, down(here, STEP_LANES), preferred_element_type=F32
            )
            piece = jnp.sum(normed_grad * normed, axis=0, keepdims=True)
            gain_out[0:1, lanes] = gain_total[0:1, lanes] + pick_0 * piece
            gain_out[1:2, lanes] = gain_total[1:2, lanes] + pick_1 * piece
    latent = lax.dot_general(
        scaled[...], down(0, 2 * width), CONTRACT_LAST, preferred_element_type=F32
    ).astype(BF16)
    for start in starts:
        lanes = slice(start, start + STEP_LANES)
        update = jnp.dot(latent, up(start, STEP_LANES), preferred_element_type=F32)
        wide = hidden[:, lanes].astype(F32)
        state_out[:, lanes] = jnp.where(active > 0.5, wide + update, wide).astype(BF16)
        grad = lax.dot_general(
            latent, cot[:, lanes], CONTRACT_FIRST, preferred_element_type=F32
        )
        grad_out[:, lanes] = (active * grad).astype(BF16)


def layer(own, hidden, embed, cot, gain, gain_total, *weights):
    rows, width = hidden.shape
    rank = weights[0].shape[2] if own else 2 * weights[0].shape[0]
    return pl.pallas_call(
        functools.partial(layer_kernel, own),
        out_shape=(
            jax.ShapeDtypeStruct((rows, width), BF16),
            jax.ShapeDtypeStruct((rank, width), BF16),
            jax.ShapeDtypeStruct(gain.shape, F32),
        ),
        scratch_shapes=[pltpu.VMEM((rows, 2 * width), BF16)],
        name="layer_own" if own else "layer_sent",
    )(hidden, embed, cot, gain, gain_total, *weights)


def exchange(array, axes):
    return lax.all_to_all(array, axes, 0, 0)


def everyone(array, axes, count):
    return exchange(jnp.broadcast_to(array[None], (count,) + array.shape), axes)


def two_parts(wide):
    high = lax.reduce_precision(wide, 8, 7)
    return high, wide - high


def on_device(
    n_xh, n_y, n_z, n_xl, n_core, hidden_input_rows, embeddings, down, up, gain, plan, cotangent
):
    sections = n_xl * n_core
    position = lax.axis_index("xl") * n_core + lax.axis_index("core")
    hidden, embed, cot = hidden_input_rows[0], embeddings[0], cotangent[0]
    rows, width = hidden.shape
    slots, rank = down.shape[1], down.shape[2]
    half = rank // 2
    blocks = gain.shape[0]
    ring = ("xh", "xl", "core")

    def weights_route(shift, side):
        route = []
        for xh in range(n_xh):
            for s in range(sections):
                source = (s + shift) % sections
                other = side and source // n_core != s // n_core
                from_xh = (xh + 1) % n_xh if other else xh
                route.append((from_xh * sections + source, xh * sections + s))
        return route

    def section_route(shift):
        return [
            (xh * sections + s, xh * sections + (s + shift) % sections)
            for xh in range(n_xh)
            for s in range(sections)
        ]

    ids = plan[0].astype(BF16)
    arrived = []
    for shift in range(1, sections):
        slot = (position < shift).astype(jnp.int32)
        id_now = jnp.broadcast_to(lax.dynamic_index_in_dim(ids, slot, 0), (half, ID_LANES))
        sides = []
        for side in range(2):
            cut = slice(side * half, (side + 1) * half)
            packet = jnp.concatenate(
                [
                    lax.dynamic_index_in_dim(down[0, :, cut], slot, 0, keepdims=False),
                    lax.dynamic_index_in_dim(up[0, :, cut], slot, 0, keepdims=False),
                    id_now,
                ],
                axis=1,
            )
            sides.append(lax.ppermute(packet, ring, weights_route(shift, side)))
        arrived.append(sides)

    own_id = jnp.broadcast_to(plan[0, 0].astype(F32), (1, ID_LANES))
    state, grad, gain_total = layer(
        True, hidden, embed, cot, gain, jnp.zeros(gain.shape, F32), down, up, own_id
    )
    wide = grad.astype(F32)
    totals = [wide, jnp.zeros_like(wide)]
    sent = []
    for shift in range(1, sections):
        state, grad, gain_total = layer(
            False, state, embed, cot, gain, gain_total, *arrived[shift - 1]
        )
        sent.append(lax.ppermute(grad, ring, section_route(shift)))
    final_rows = lax.ppermute(state, ring, section_route(-1))
    for shift, grad in enumerate(sent, 1):
        late = position < shift
        wide = grad.astype(F32)
        totals[0] = totals[0] + jnp.where(late, 0.0, wide)
        totals[1] = totals[1] + jnp.where(late, wide, 0.0)

    near = n_xh * n_y
    deep = slots * rank // near
    gain_lanes = gain.size // (near * deep)
    room = -(-gain_lanes // 128) * 128
    lanes = width + 2 * room
    grads = jnp.stack(totals).reshape(near, deep, width)

    def with_gain(grads, gains):
        pad = [(0, 0)] * (gains.ndim - 1) + [(0, room - gains.shape[-1])]
        parts = [jnp.pad(x, pad) for x in two_parts(gains)]
        return jnp.concatenate([grads] + parts, axis=-1).astype(BF16)

    packet = with_gain(grads, gain_total.reshape(near, deep, gain_lanes))
    total = jnp.sum(exchange(packet, ("xh", "y")).astype(F32), axis=0)
    packet = with_gain(
        total[:, :width], total[:, width : width + room] + total[:, width + room :]
    )
    tiles = lanes // 128
    chunk = deep * tiles // n_z
    packet = packet.reshape(n_z, chunk, 128)
    total = jnp.sum(exchange(packet, "z").astype(F32), axis=0)
    over_sections = jnp.sum(everyone(total, ("xl", "core"), sections), axis=0)
    tile = (lax.axis_index("z") * chunk + jnp.arange(chunk)) % tiles
    total = jnp.where((tile * 128 >= width)[:, None], over_sections, total)
    total = everyone(total.astype(BF16), "z", n_z).reshape(deep, lanes)
    total = everyone(total, ("xh", "y"), near).astype(F32)
    scale = 1.0 / math.sqrt(rows * n_xh * n_y * n_z)
    lora = (total[:, :, :width] * scale).reshape(1, slots, rank, width)
    gains = total[:, :, width : width + gain_lanes]
    gains = gains + total[:, :, width + room : width + room + gain_lanes]
    return final_rows[None], lora, (gains * scale).reshape(gain.shape)


def solution(mesh):
    n_dp, sections = mesh.devices.shape
    n_z, n_xh, n_xl = 12, 2, 2
    n_y, n_core = n_dp // (n_z * n_xh), sections // n_xl
    fine = Mesh(
        np.asarray(mesh.devices).reshape(n_z, n_xh, n_y, n_xl, n_core),
        ("z", "xh", "y", "xl", "core"),
    )
    dp, section = ("z", "xh", "y"), ("xl", "core")
    rows = P(section, dp, None)
    weights = P(section, None, None, None)
    return jax.shard_map(
        functools.partial(on_device, n_xh, n_y, n_z, n_xl, n_core),
        mesh=fine,
        in_specs=(rows, rows, weights, weights, P(), P(section, None), rows),
        out_specs=(rows, weights, P()),
        check_vma=False,
    )
```

```python
import functools
import math

import jax
import jax.numpy as jnp
import numpy as np
from jax import lax
from jax.experimental import pallas as pl
from jax.experimental.pallas import tpu as pltpu
from jax.sharding import Mesh
from jax.sharding import PartitionSpec as P


F32 = jnp.float32
BF16 = jnp.bfloat16
STEP_LANES = 512
ID_LANES = 128
CONTRACT_LAST = (((1,), (1,)), ((), ()))
CONTRACT_FIRST = (((0,), (0,)), ((), ()))


def layer_kernel(own, hidden, embed, cot, gain, gain_total, *refs):
    width = hidden.shape[-1]
    if own:
        down_ref, up_ref, id_ref, state_out, grad_out, gain_out, scaled = refs

        def down(start, size):
            return down_ref[0, 0, :, start : start + size]

        def up(start, size):
            return up_ref[0, 0, :, start : start + size]

        ids = id_ref[...]
    else:
        first, second, state_out, grad_out, gain_out, scaled = refs

        def down(start, size):
            return jnp.concatenate(
                [first[:, start : start + size], second[:, start : start + size]], axis=0
            )

        def up(start, size):
            return down(2 * width + start, size)

        ids = first[0:1, 3 * width : 3 * width + ID_LANES].astype(F32)
    block_id = jnp.max(ids, axis=1, keepdims=True)
    pick_0 = (jnp.abs(block_id - 0.0) < 0.5).astype(F32)
    pick_1 = (jnp.abs(block_id - 1.0) < 0.5).astype(F32)
    active = pick_0 + pick_1

    starts = range(0, width, STEP_LANES)
    squares = jnp.zeros((hidden.shape[0], ID_LANES), F32)
    for rows in (hidden, embed):
        for start in starts:
            wide = rows[:, start : start + STEP_LANES].astype(F32)
            wide = wide * wide
            for lane in range(0, STEP_LANES, ID_LANES):
                squares = squares + wide[:, lane : lane + ID_LANES]
    squares_sum = jnp.sum(squares, axis=1, keepdims=True)
    inverse = lax.rsqrt(squares_sum / (2 * width) + 1e-05)

    latent_grad = lax.dot_general(
        cot[...], up(0, width), CONTRACT_LAST, preferred_element_type=F32
    ).astype(BF16)
    for part, rows in enumerate((hidden, embed)):
        for start in starts:
            here = part * width + start
            lanes = slice(here, here + STEP_LANES)
            normed = rows[:, start : start + STEP_LANES].astype(F32) * inverse
            gain_now = pick_0 * gain[0:1, lanes] + pick_1 * gain[1:2, lanes]
            scaled[:, lanes] = (normed * gain_now).astype(BF16)
            normed_grad = jnp.dot(
                latent_grad, down(here, STEP_LANES), preferred_element_type=F32
            )
            piece = jnp.sum(normed_grad * normed, axis=0, keepdims=True)
            gain_out[0:1, lanes] = gain_total[0:1, lanes] + pick_0 * piece
            gain_out[1:2, lanes] = gain_total[1:2, lanes] + pick_1 * piece
    latent = lax.dot_general(
        scaled[...], down(0, 2 * width), CONTRACT_LAST, preferred_element_type=F32
    ).astype(BF16)
    for start in starts:
        lanes = slice(start, start + STEP_LANES)
        update = jnp.dot(latent, up(start, STEP_LANES), preferred_element_type=F32)
        wide = hidden[:, lanes].astype(F32)
        state_out[:, lanes] = jnp.where(active > 0.5, wide + update, wide).astype(BF16)
        grad = lax.dot_general(
            latent, cot[:, lanes], CONTRACT_FIRST, preferred_element_type=F32
        )
        grad_out[:, lanes] = (active * grad).astype(BF16)


def layer(own, hidden, embed, cot, gain, gain_total, *weights):
    rows, width = hidden.shape
    rank = weights[0].shape[2] if own else 2 * weights[0].shape[0]
    return pl.pallas_call(
        functools.partial(layer_kernel, own),
        out_shape=(
            jax.ShapeDtypeStruct((rows, width), BF16),
            jax.ShapeDtypeStruct((rank, width), BF16),
            jax.ShapeDtypeStruct(gain.shape, F32),
        ),
        scratch_shapes=[pltpu.VMEM((rows, 2 * width), BF16)],
        name="layer_own" if own else "layer_sent",
    )(hidden, embed, cot, gain, gain_total, *weights)


def pack_kernel(slot, down, up, ids, *packets):
    width, half = up.shape[-1], packets[0].shape[0]
    here = slot[0]
    block_id = jnp.where(here == 0, ids[0], ids[1])
    for side, packet in enumerate(packets):
        rows = slice(side * half, (side + 1) * half)
        packet[:, : 2 * width] = down[0, 0, rows, :]
        packet[:, 2 * width : 3 * width] = up[0, 0, rows, :]
        packet[:, 3 * width :] = jnp.full((half, ID_LANES), block_id, F32).astype(BF16)


def pack(slot, down, up, ids):
    rank, width = up.shape[2:]
    half = rank // 2
    packet = jax.ShapeDtypeStruct((half, 3 * width + ID_LANES), BF16)
    whole = pl.BlockSpec(packet.shape, lambda i, slot: (0, 0))
    return pl.pallas_call(
        pack_kernel,
        out_shape=(packet, packet),
        grid_spec=pltpu.PrefetchScalarGridSpec(
            num_scalar_prefetch=1,
            grid=(1,),
            in_specs=[
                pl.BlockSpec((1, 1, rank, 2 * width), lambda i, slot: (0, slot[0], 0, 0)),
                pl.BlockSpec((1, 1, rank, width), lambda i, slot: (0, slot[0], 0, 0)),
                pl.BlockSpec(memory_space=pltpu.SMEM),
            ],
            out_specs=(whole, whole),
        ),
        name="pack",
    )(slot, down, up, ids)


def exchange(array, axes):
    return lax.all_to_all(array, axes, 0, 0)


def everyone(array, axes, count):
    return exchange(jnp.broadcast_to(array[None], (count,) + array.shape), axes)


def two_parts(wide):
    high = lax.reduce_precision(wide, 8, 7)
    return high, wide - high


def on_device(
    n_xh, n_y, n_z, n_xl, n_core, hidden_input_rows, embeddings, down, up, gain, plan, cotangent
):
    sections = n_xl * n_core
    position = lax.axis_index("xl") * n_core + lax.axis_index("core")
    hidden, embed, cot = hidden_input_rows[0], embeddings[0], cotangent[0]
    rows, width = hidden.shape
    slots, rank = down.shape[1], down.shape[2]
    ring = ("xh", "xl", "core")

    def weights_route(shift, side):
        route = []
        for xh in range(n_xh):
            for s in range(sections):
                source = (s + shift) % sections
                other = side and source // n_core != s // n_core
                from_xh = (xh + 1) % n_xh if other else xh
                route.append((from_xh * sections + source, xh * sections + s))
        return route

    def section_route(shift):
        return [
            (xh * sections + s, xh * sections + (s + shift) % sections)
            for xh in range(n_xh)
            for s in range(sections)
        ]

    ids = plan[0].astype(F32)
    arrived = []
    for shift in range(1, sections):
        slot = (position < shift).astype(jnp.int32).reshape(1)
        packets = pack(slot, down, up, ids)
        sides = []
        for side in range(2):
            sides.append(lax.ppermute(packets[side], ring, weights_route(shift, side)))
        arrived.append(sides)

    own_id = jnp.broadcast_to(ids[0], (1, ID_LANES))
    state, grad, gain_total = layer(
        True, hidden, embed, cot, gain, jnp.zeros(gain.shape, F32), down, up, own_id
    )
    wide = grad.astype(F32)
    totals = [wide, jnp.zeros_like(wide)]
    sent = []
    for shift in range(1, sections):
        state, grad, gain_total = layer(
            False, state, embed, cot, gain, gain_total, *arrived[shift - 1]
        )
        sent.append(lax.ppermute(grad, ring, section_route(shift)))
    gain_total = jnp.sum(everyone(gain_total, ("xl", "core"), sections), axis=0)
    final_rows = lax.ppermute(state, ring, section_route(-1))
    for shift, grad in enumerate(sent, 1):
        late = position < shift
        wide = grad.astype(F32)
        totals[0] = totals[0] + jnp.where(late, 0.0, wide)
        totals[1] = totals[1] + jnp.where(late, wide, 0.0)

    near = n_xh * n_y
    deep = slots * rank // near
    gain_lanes = gain.size // (near * deep)
    room = -(-gain_lanes // 128) * 128
    lanes = width + 2 * room
    grads = jnp.stack(totals).reshape(near, deep, width)

    def with_gain(grads, gains):
        pad = [(0, 0)] * (gains.ndim - 1) + [(0, room - gains.shape[-1])]
        parts = [jnp.pad(x, pad) for x in two_parts(gains)]
        return jnp.concatenate([grads] + parts, axis=-1).astype(BF16)

    packet = with_gain(grads, gain_total.reshape(near, deep, gain_lanes))
    packet = exchange(packet, ("xh", "y"))
    total = jnp.sum(packet.astype(F32), axis=0)
    packet = with_gain(
        total[:, :width], total[:, width : width + room] + total[:, width + room :]
    )
    packet = packet.reshape(n_z, deep * lanes // 128 // n_z, 128)
    packet = exchange(packet, "z")
    total = jnp.sum(packet.astype(F32), axis=0).astype(BF16)
    total = everyone(total, "z", n_z)
    total = total.reshape(deep, lanes)
    total = everyone(total, ("xh", "y"), near)
    total = total.astype(F32)
    scale = 1.0 / math.sqrt(rows * n_xh * n_y * n_z)
    lora = (total[:, :, :width] * scale).reshape(1, slots, rank, width)
    gains = total[:, :, width : width + gain_lanes]
    gains = gains + total[:, :, width + room : width + room + gain_lanes]
    return final_rows[None], lora, (gains * scale).reshape(gain.shape)


def solution(mesh):
    n_dp, sections = mesh.devices.shape
    n_z, n_xh, n_xl = 12, 2, 2
    n_y, n_core = n_dp // (n_z * n_xh), sections // n_xl
    fine = Mesh(
        np.asarray(mesh.devices).reshape(n_z, n_xh, n_y, n_xl, n_core),
        ("z", "xh", "y", "xl", "core"),
    )
    dp, section = ("z", "xh", "y"), ("xl", "core")
    rows = P(section, dp, None)
    weights = P(section, None, None, None)
    return jax.shard_map(
        functools.partial(on_device, n_xh, n_y, n_z, n_xl, n_core),
        mesh=fine,
        in_specs=(rows, rows, weights, weights, P(), P(section, None), rows),
        out_specs=(rows, weights, P()),
        check_vma=False,
    )
```

```python
import functools
import math

import jax
import jax.numpy as jnp
import numpy as np
from jax import lax
from jax.experimental import pallas as pl
from jax.experimental.pallas import tpu as pltpu
from jax.sharding import Mesh
from jax.sharding import PartitionSpec as P


F32 = jnp.float32
BF16 = jnp.bfloat16
STEP_LANES = 512
ID_LANES = 128
CONTRACT_LAST = (((1,), (1,)), ((), ()))
CONTRACT_FIRST = (((0,), (0,)), ((), ()))


def layer_kernel(own, *refs):
    if own:
        plan, hidden_in, embed_in, cot_in, gain, down_in, up_in = refs[:7]
        rest = refs[7:]
        gain_total = None
    else:
        hidden_in, embed_in, cot_in, gain, gain_total, first, second = refs[:7]
        rest = refs[7:]
    state_out, grad_out, gain_out, hidden, embed, cot, down, up, ids, scaled, sems = rest
    rows, width = hidden.shape
    half = down.shape[0] // 2
    moves = [(hidden_in, hidden), (embed_in, embed), (cot_in, cot)]
    if own:
        moves += [(up_in.at[0, 0], up), (down_in.at[0, 0], down)]
    else:
        for side, packet in enumerate((first, second)):
            part = pl.ds(side * half, half)
            moves.append((packet.at[:, pl.ds(2 * width, width)], up.at[part]))
        moves.append((first.at[:, pl.ds(3 * width, ID_LANES)], ids))
        for side, packet in enumerate((first, second)):
            part = pl.ds(side * half, half)
            moves.append((packet.at[:, pl.ds(0, 2 * width)], down.at[part]))
    copies = [
        pltpu.make_async_copy(source, target, sems.at[i])
        for i, (source, target) in enumerate(moves)
    ]
    for copy in copies:
        copy.start()

    starts = range(0, width, STEP_LANES)
    squares = jnp.zeros((rows, ID_LANES), F32)
    for copy, source in zip(copies[:2], (hidden, embed)):
        copy.wait()
        for start in starts:
            wide = source[:, start : start + STEP_LANES].astype(F32)
            wide = wide * wide
            for lane in range(0, STEP_LANES, ID_LANES):
                squares = squares + wide[:, lane : lane + ID_LANES]
    squares_sum = jnp.sum(squares, axis=1, keepdims=True)
    inverse = lax.rsqrt(squares_sum / (2 * width) + 1e-05)

    for copy in copies[2 : 4 if own else 6]:
        copy.wait()
    if own:
        block_id = jnp.full((1, 1), plan[0, 0], jnp.int32).astype(F32)
    else:
        block_id = jnp.max(ids[0:1, :].astype(F32), axis=1, keepdims=True)
    pick_0 = (jnp.abs(block_id - 0.0) < 0.5).astype(F32)
    pick_1 = (jnp.abs(block_id - 1.0) < 0.5).astype(F32)
    active = pick_0 + pick_1
    latent_grad = lax.dot_general(
        cot[...], up[...], CONTRACT_LAST, preferred_element_type=F32
    ).astype(BF16)
    for copy in copies[4 if own else 6 :]:
        copy.wait()
    for part, source in enumerate((hidden, embed)):
        for start in starts:
            here = part * width + start
            lanes = slice(here, here + STEP_LANES)
            normed = source[:, start : start + STEP_LANES].astype(F32) * inverse
            gain_now = pick_0 * gain[0:1, lanes] + pick_1 * gain[1:2, lanes]
            scaled[:, lanes] = (normed * gain_now).astype(BF16)
            normed_grad = jnp.dot(latent_grad, down[:, lanes], preferred_element_type=F32)
            piece = jnp.sum(normed_grad * normed, axis=0, keepdims=True)
            for block, pick in enumerate((pick_0, pick_1)):
                row = slice(block, block + 1)
                total = pick * piece
                if not own:
                    total = gain_total[row, lanes] + total
                gain_out[row, lanes] = total
    latent = lax.dot_general(
        scaled[...], down[...], CONTRACT_LAST, preferred_element_type=F32
    ).astype(BF16)
    for start in starts:
        lanes = slice(start, start + STEP_LANES)
        update = jnp.dot(latent, up[:, lanes], preferred_element_type=F32)
        wide = hidden[:, lanes].astype(F32)
        state_out[:, lanes] = jnp.where(active > 0.5, wide + update, wide).astype(BF16)
        grad = lax.dot_general(
            latent, cot[:, lanes], CONTRACT_FIRST, preferred_element_type=F32
        )
        grad_out[:, lanes] = (active * grad).astype(BF16)


HBM = pl.BlockSpec(memory_space=pltpu.HBM)
SMEM = pl.BlockSpec(memory_space=pltpu.SMEM)
VMEM = pl.BlockSpec(memory_space=pltpu.VMEM)


def layer(hidden, embed, cot, gain, gain_total, weights, plan=None):
    own = plan is not None
    rows, width = hidden.shape
    rank = weights[0].shape[2] if own else 2 * weights[0].shape[0]
    if own:
        args = (plan, hidden, embed, cot, gain, *weights)
        specs = (SMEM, HBM, HBM, HBM, VMEM, HBM, HBM)
    else:
        args = (hidden, embed, cot, gain, gain_total, *weights)
        specs = (HBM, HBM, HBM, VMEM, VMEM, HBM, HBM)
    return pl.pallas_call(
        functools.partial(layer_kernel, own),
        out_shape=(
            jax.ShapeDtypeStruct((rows, width), BF16),
            jax.ShapeDtypeStruct((rank, width), BF16),
            jax.ShapeDtypeStruct(gain.shape, F32),
        ),
        in_specs=specs,
        scratch_shapes=[
            pltpu.VMEM((rows, width), BF16),
            pltpu.VMEM((rows, width), BF16),
            pltpu.VMEM((rows, width), BF16),
            pltpu.VMEM((rank, 2 * width), BF16),
            pltpu.VMEM((rank, width), BF16),
            pltpu.VMEM((rank // 2, ID_LANES), BF16),
            pltpu.VMEM((rows, 2 * width), BF16),
            pltpu.SemaphoreType.DMA((8,)),
        ],
        compiler_params=pltpu.CompilerParams(vmem_limit_bytes=66846720),
        name="layer_own" if own else "layer_sent",
    )(*args)


def pack_kernel(slot, plan, down, up, first, second, ids, sems):
    half, width = first.shape[0], up.shape[-1]
    here = slot[0]
    copies = []
    for side, packet in enumerate((first, second)):
        part = pl.ds(side * half, half)
        copies.append((down.at[0, here, part], packet.at[:, pl.ds(0, 2 * width)]))
        copies.append((up.at[0, here, part], packet.at[:, pl.ds(2 * width, width)]))
    block_id = jnp.where(here == 0, plan[0, 0], plan[0, 1])
    ids[...] = jnp.full(ids.shape, block_id, jnp.int32).astype(F32).astype(BF16)
    for packet in (first, second):
        copies.append((ids, packet.at[:, pl.ds(3 * width, ID_LANES)]))
    copies = [pltpu.make_async_copy(a, b, sems.at[i]) for i, (a, b) in enumerate(copies)]
    for copy in copies:
        copy.start()
    for copy in copies:
        copy.wait()


def pack(slot, plan, down, up):
    rank, width = up.shape[2:]
    packet = jax.ShapeDtypeStruct((rank // 2, 3 * width + ID_LANES), BF16)
    return pl.pallas_call(
        pack_kernel,
        out_shape=(packet, packet),
        in_specs=(SMEM, SMEM, HBM, HBM),
        out_specs=(HBM, HBM),
        scratch_shapes=[
            pltpu.VMEM((rank // 2, ID_LANES), BF16),
            pltpu.SemaphoreType.DMA((6,)),
        ],
        name="pack",
    )(slot, plan, down, up)


def exchange(array, axes):
    return lax.all_to_all(array, axes, 0, 0)


def everyone(array, axes, count):
    return exchange(jnp.broadcast_to(array[None], (count,) + array.shape), axes)


def two_parts(wide):
    high = lax.reduce_precision(wide, 8, 7)
    return high, wide - high


def on_device(
    n_z_hi, n_z_lo, n_xh, n_y, n_xl, n_core, hidden_input_rows, embeddings, down, up, gain, plan, cotangent
):
    sections = n_xl * n_core
    position = lax.axis_index("xl") * n_core + lax.axis_index("core")
    hidden, embed, cot = hidden_input_rows[0], embeddings[0], cotangent[0]
    rows, width = hidden.shape
    slots, rank = down.shape[1], down.shape[2]
    ring = ("xh", "xl", "core")

    def weights_route(shift, side):
        route = []
        for xh in range(n_xh):
            for s in range(sections):
                source = (s + shift) % sections
                other = side and source // n_core != s // n_core
                from_xh = (xh + 1) % n_xh if other else xh
                route.append((from_xh * sections + source, xh * sections + s))
        return route

    def section_route(shift):
        return [
            (xh * sections + s, xh * sections + (s + shift) % sections)
            for xh in range(n_xh)
            for s in range(sections)
        ]

    arrived = []
    for shift in range(1, sections):
        slot = (position < shift).astype(jnp.int32).reshape(1)
        packets = pack(slot, plan, down, up)
        sides = []
        for side in range(2):
            sides.append(lax.ppermute(packets[side], ring, weights_route(shift, side)))
        arrived.append(sides)

    state, grad, gain_total = layer(
        hidden, embed, cot, gain, None, (down, up), plan
    )
    wide = grad.astype(F32)
    totals = [wide, jnp.zeros_like(wide)]
    sent = []
    for shift in range(1, sections):
        state, grad, gain_total = layer(
            state, embed, cot, gain, gain_total, arrived[shift - 1]
        )
        sent.append(lax.ppermute(grad, ring, section_route(shift)))
    gain_total = jnp.sum(everyone(gain_total, ("xl", "core"), sections), axis=0)
    final_rows = lax.ppermute(state, ring, section_route(-1))
    for shift, grad in enumerate(sent, 1):
        late = position < shift
        wide = grad.astype(F32)
        totals[0] = totals[0] + jnp.where(late, 0.0, wide)
        totals[1] = totals[1] + jnp.where(late, wide, 0.0)

    near = n_xh * n_y
    deep = slots * rank // near
    gain_lanes = gain.size // (near * deep)
    room = -(-gain_lanes // 128) * 128
    grads = jnp.stack(totals).reshape(near, deep, width)

    def with_gain(grads, gains):
        pad = [(0, 0)] * (gains.ndim - 1) + [(0, room - gains.shape[-1])]
        parts = [jnp.pad(x, pad) for x in two_parts(gains)]
        return jnp.concatenate([grads] + parts, axis=-1).astype(BF16)

    packet = with_gain(grads, gain_total.reshape(near, deep, gain_lanes))
    packet = exchange(packet, ("xh", "y"))
    total = jnp.sum(packet.astype(F32), axis=0)
    for axis, count in (("z_lo", n_z_lo), ("z_hi", n_z_hi)):
        packet = with_gain(
            total[:, :width], total[:, width : width + room] + total[:, width + room :]
        )
        packet = everyone(packet, axis, count)
        total = jnp.sum(packet.astype(F32), axis=0)
    total = with_gain(
        total[:, :width], total[:, width : width + room] + total[:, width + room :]
    )
    total = everyone(total, ("xh", "y"), near)
    total = total.astype(F32)
    scale = 1.0 / math.sqrt(rows * n_xh * n_y * n_z_hi * n_z_lo)
    lora = (total[:, :, :width] * scale).reshape(1, slots, rank, width)
    gains = total[:, :, width : width + gain_lanes]
    gains = gains + total[:, :, width + room : width + room + gain_lanes]
    return final_rows[None], lora, (gains * scale).reshape(gain.shape)


def solution(mesh):
    n_dp, sections = mesh.devices.shape
    n_z_hi, n_z_lo, n_xh, n_xl = 3, 4, 2, 2
    n_y, n_core = n_dp // (n_z_hi * n_z_lo * n_xh), sections // n_xl
    sizes = (n_z_hi, n_z_lo, n_xh, n_y, n_xl, n_core)
    dp, section = ("z_hi", "z_lo", "xh", "y"), ("xl", "core")
    fine = Mesh(np.asarray(mesh.devices).reshape(sizes), dp + section)
    rows = P(section, dp, None)
    weights = P(section, None, None, None)
    return jax.shard_map(
        functools.partial(on_device, *sizes),
        mesh=fine,
        in_specs=(rows, rows, weights, weights, P(), P(section, None), rows),
        out_specs=(rows, weights, P()),
        check_vma=False,
    )
```

```python
import functools
import math

import jax
import jax.numpy as jnp
import numpy as np
from jax import lax
from jax.experimental import pallas as pl
from jax.experimental.pallas import tpu as pltpu
from jax.sharding import Mesh
from jax.sharding import PartitionSpec as P


F32 = jnp.float32
BF16 = jnp.bfloat16
STEP_LANES = 512
ID_LANES = 128
CONTRACT_LAST = (((1,), (1,)), ((), ()))


def layer_kernel(own, *refs):
    if own:
        plan, hidden_in, embed_in, cot_in, gain, down_in, up_in = refs[:7]
        state_out, grad_out, gain_out, squares_ref, *rest = refs[7:]
        gain_total = None
    else:
        hidden_in, embed_in, cot_in, gain, gain_total, squares_ref, first, second = refs[:8]
        state_out, grad_out, gain_out, *rest = refs[8:]
    hidden, embed, cot, down, up, ids, scaled, sems = rest
    rows, width = hidden.shape
    half = down.shape[0] // 2
    moves = [(hidden_in, hidden), (embed_in, embed), (cot_in, cot)]
    if own:
        moves += [(up_in.at[0, 0], up), (down_in.at[0, 0], down)]
    else:
        for side, packet in enumerate((first, second)):
            part = pl.ds(side * half, half)
            moves.append((packet.at[:, pl.ds(2 * width, width)], up.at[part]))
        moves.append((first.at[:, pl.ds(3 * width, ID_LANES)], ids))
        for side, packet in enumerate((first, second)):
            part = pl.ds(side * half, half)
            moves.append((packet.at[:, pl.ds(0, 2 * width)], down.at[part]))
    copies = [
        pltpu.make_async_copy(source, target, sems.at[i])
        for i, (source, target) in enumerate(moves)
    ]
    for copy in copies:
        copy.start()

    starts = range(0, width, STEP_LANES)

    def squares_of(source):
        squares = jnp.zeros((rows, ID_LANES), F32)
        for start in starts:
            wide = source[:, start : start + STEP_LANES].astype(F32)
            wide = wide * wide
            for lane in range(0, STEP_LANES, ID_LANES):
                squares = squares + wide[:, lane : lane + ID_LANES]
        return squares

    copies[0].wait()
    squares = squares_of(hidden)
    copies[1].wait()
    if own:
        squares_ref[...] = squares_of(embed)
    squares = squares + squares_ref[...]
    squares_sum = jnp.sum(squares, axis=1, keepdims=True)
    inverse = lax.rsqrt(squares_sum / (2 * width) + 1e-05)

    for copy in copies[2 : 4 if own else 6]:
        copy.wait()
    if own:
        block_id = jnp.full((1, 1), plan[0, 0], jnp.int32).astype(F32)
    else:
        block_id = jnp.max(ids[0:1, :].astype(F32), axis=1, keepdims=True)
    pick_0 = (jnp.abs(block_id - 0.0) < 0.5).astype(F32)
    pick_1 = (jnp.abs(block_id - 1.0) < 0.5).astype(F32)
    active = pick_0 + pick_1
    latent_grad = lax.dot_general(
        cot[...], up[...], CONTRACT_LAST, preferred_element_type=F32
    ).astype(BF16)
    for copy in copies[4 if own else 6 :]:
        copy.wait()
    for part, source in enumerate((hidden, embed)):
        for start in starts:
            here = part * width + start
            lanes = slice(here, here + STEP_LANES)
            normed = source[:, start : start + STEP_LANES].astype(F32) * inverse
            gain_now = pick_0 * gain[0:1, lanes] + pick_1 * gain[1:2, lanes]
            scaled[:, lanes] = (normed * gain_now).astype(BF16)
            normed_grad = jnp.dot(latent_grad, down[:, lanes], preferred_element_type=F32)
            piece = jnp.sum(normed_grad * normed, axis=0, keepdims=True)
            for block, pick in enumerate((pick_0, pick_1)):
                row = slice(block, block + 1)
                total = pick * piece
                if not own:
                    total = gain_total[row, lanes] + total
                gain_out[row, lanes] = total
    latent = lax.dot_general(
        scaled[...], down[...], CONTRACT_LAST, preferred_element_type=F32
    ).astype(BF16)
    latent_turned = latent.astype(F32).T.astype(BF16)
    for start in starts:
        lanes = slice(start, start + STEP_LANES)
        update = jnp.dot(latent, up[:, lanes], preferred_element_type=F32)
        wide = hidden[:, lanes].astype(F32)
        state_out[:, lanes] = jnp.where(active > 0.5, wide + update, wide).astype(BF16)
        grad = jnp.dot(latent_turned, cot[:, lanes], preferred_element_type=F32)
        grad_out[:, lanes] = (active * grad).astype(BF16)


HBM = pl.BlockSpec(memory_space=pltpu.HBM)
SMEM = pl.BlockSpec(memory_space=pltpu.SMEM)
VMEM = pl.BlockSpec(memory_space=pltpu.VMEM)


def layer(hidden, embed, cot, gain, carried, weights, plan=None):
    own = plan is not None
    rows, width = hidden.shape
    rank = weights[0].shape[2] if own else 2 * weights[0].shape[0]
    if own:
        args = (plan, hidden, embed, cot, gain, *weights)
        specs = (SMEM, HBM, HBM, HBM, VMEM, HBM, HBM)
    else:
        args = (hidden, embed, cot, gain, *carried, *weights)
        specs = (HBM, HBM, HBM, VMEM, VMEM, VMEM, HBM, HBM)
    return pl.pallas_call(
        functools.partial(layer_kernel, own),
        out_shape=(
            jax.ShapeDtypeStruct((rows, width), BF16),
            jax.ShapeDtypeStruct((rank, width), BF16),
            jax.ShapeDtypeStruct(gain.shape, F32),
        )
        + ((jax.ShapeDtypeStruct((rows, ID_LANES), F32),) if own else ()),
        in_specs=specs,
        scratch_shapes=[
            pltpu.VMEM((rows, width), BF16),
            pltpu.VMEM((rows, width), BF16),
            pltpu.VMEM((rows, width), BF16),
            pltpu.VMEM((rank, 2 * width), BF16),
            pltpu.VMEM((rank, width), BF16),
            pltpu.VMEM((rank // 2, ID_LANES), BF16),
            pltpu.VMEM((rows, 2 * width), BF16),
            pltpu.SemaphoreType.DMA((8,)),
        ],
        compiler_params=pltpu.CompilerParams(vmem_limit_bytes=66846720),
        name="layer_own" if own else "layer_sent",
    )(*args)


def pack_kernel(slot, down, up, plan, *packets):
    width, half = up.shape[-1], packets[0].shape[0]
    block_id = jnp.where(slot[0] == 0, plan[0, 0], plan[0, 1])
    for side, packet in enumerate(packets):
        rows = slice(side * half, (side + 1) * half)
        packet[:, : 2 * width] = down[0, 0, rows, :]
        packet[:, 2 * width : 3 * width] = up[0, 0, rows, :]
        ids = jnp.full((half, ID_LANES), block_id, jnp.int32)
        packet[:, 3 * width :] = ids.astype(F32).astype(BF16)


def pack(slot, plan, down, up):
    rank, width = up.shape[2:]
    packet = jax.ShapeDtypeStruct((rank // 2, 3 * width + ID_LANES), BF16)
    whole = pl.BlockSpec(packet.shape, lambda i, slot: (0, 0))
    return pl.pallas_call(
        pack_kernel,
        out_shape=(packet, packet),
        grid_spec=pltpu.PrefetchScalarGridSpec(
            num_scalar_prefetch=1,
            grid=(1,),
            in_specs=[
                pl.BlockSpec((1, 1, rank, 2 * width), lambda i, slot: (0, slot[0], 0, 0)),
                pl.BlockSpec((1, 1, rank, width), lambda i, slot: (0, slot[0], 0, 0)),
                SMEM,
            ],
            out_specs=(whole, whole),
        ),
        name="pack",
    )(slot, down, up, plan)


def exchange(array, axes):
    return lax.all_to_all(array, axes, 0, 0)


def everyone(array, axes, count):
    return exchange(jnp.broadcast_to(array[None], (count,) + array.shape), axes)


def two_parts(wide):
    high = lax.reduce_precision(wide, 8, 7)
    return high, wide - high


def on_device(
    n_z_hi, n_z_lo, n_xh, n_y, n_xl, n_core, hidden_input_rows, embeddings, down, up, gain, plan, cotangent
):
    sections = n_xl * n_core
    position = lax.axis_index("xl") * n_core + lax.axis_index("core")
    hidden, embed, cot = hidden_input_rows[0], embeddings[0], cotangent[0]
    rows, width = hidden.shape
    slots, rank = down.shape[1], down.shape[2]
    ring = ("xh", "xl", "core")

    def weights_route(shift, side):
        route = []
        for xh in range(n_xh):
            for s in range(sections):
                source = (s + shift) % sections
                other = side and source // n_core != s // n_core
                from_xh = (xh + 1) % n_xh if other else xh
                route.append((from_xh * sections + source, xh * sections + s))
        return route

    def section_route(shift):
        return [
            (xh * sections + s, xh * sections + (s + shift) % sections)
            for xh in range(n_xh)
            for s in range(sections)
        ]

    arrived = []
    for shift in range(1, sections):
        slot = (position < shift).astype(jnp.int32).reshape(1)
        packets = pack(slot, plan, down, up)
        sides = []
        for side in range(2):
            sides.append(lax.ppermute(packets[side], ring, weights_route(shift, side)))
        arrived.append(sides)

    state, grad, gain_total, squares = layer(
        hidden, embed, cot, gain, (), (down, up), plan
    )
    wide = grad.astype(F32)
    totals = [wide, jnp.zeros_like(wide)]
    sent = []
    for shift in range(1, sections):
        state, grad, gain_total = layer(
            state, embed, cot, gain, (gain_total, squares), arrived[shift - 1]
        )
        sent.append(lax.ppermute(grad, ring, section_route(shift)))
    gain_total = jnp.sum(everyone(gain_total, ("xl", "core"), sections), axis=0)
    final_rows = lax.ppermute(state, ring, section_route(-1))
    for shift, grad in enumerate(sent, 1):
        late = position < shift
        wide = grad.astype(F32)
        totals[0] = totals[0] + jnp.where(late, 0.0, wide)
        totals[1] = totals[1] + jnp.where(late, wide, 0.0)

    near = n_xh * n_y
    deep = slots * rank // near
    gain_lanes = gain.size // (near * deep)
    room = -(-gain_lanes // 128) * 128
    grads = jnp.stack(totals).reshape(near, deep, width)

    def with_gain(grads, gains):
        pad = [(0, 0)] * (gains.ndim - 1) + [(0, room - gains.shape[-1])]
        parts = [jnp.pad(x, pad) for x in two_parts(gains)]
        return jnp.concatenate([grads] + parts, axis=-1).astype(BF16)

    packet = with_gain(grads, gain_total.reshape(near, deep, gain_lanes))
    packet = exchange(packet, ("xh", "y"))
    total = jnp.sum(packet.astype(F32), axis=0)
    for axis, count in (("z_lo", n_z_lo), ("z_hi", n_z_hi)):
        packet = with_gain(
            total[:, :width], total[:, width : width + room] + total[:, width + room :]
        )
        packet = everyone(packet, axis, count)
        total = jnp.sum(packet.astype(F32), axis=0)
    total = with_gain(
        total[:, :width], total[:, width : width + room] + total[:, width + room :]
    )
    total = everyone(total, ("xh", "y"), near)
    total = total.astype(F32)
    scale = 1.0 / math.sqrt(rows * n_xh * n_y * n_z_hi * n_z_lo)
    lora = (total[:, :, :width] * scale).reshape(1, slots, rank, width)
    gains = total[:, :, width : width + gain_lanes]
    gains = gains + total[:, :, width + room : width + room + gain_lanes]
    return final_rows[None], lora, (gains * scale).reshape(gain.shape)


def solution(mesh):
    n_dp, sections = mesh.devices.shape
    n_z_hi, n_z_lo, n_xh, n_xl = 3, 4, 2, 2
    n_y, n_core = n_dp // (n_z_hi * n_z_lo * n_xh), sections // n_xl
    sizes = (n_z_hi, n_z_lo, n_xh, n_y, n_xl, n_core)
    dp, section = ("z_hi", "z_lo", "xh", "y"), ("xl", "core")
    fine = Mesh(np.asarray(mesh.devices).reshape(sizes), dp + section)
    rows = P(section, dp, None)
    weights = P(section, None, None, None)
    return jax.shard_map(
        functools.partial(on_device, *sizes),
        mesh=fine,
        in_specs=(rows, rows, weights, weights, P(), P(section, None), rows),
        out_specs=(rows, weights, P()),
        check_vma=False,
    )
```
